32 devices in a mesh: grp: 2 (over x), tm: 16 (over z, y, core).
Axes of the slice: x: 2, y: 2, z: 4, core: 2. Of those that a mesh axis runs over, the one named last changes fastest.
Arguments:
- observations: bfloat16 [65536, 1024], P(('grp', 'tm')), parts along dimension 0, may hold values from -0.1875 to 0.1875
- counts: int32 [32], P(('grp', 'tm')), parts along dimension 0, may hold values from 1 to 2048, 10922 in all
- prior: float32 [32, 1024], P(('grp', 'tm')), parts along dimension 0, may hold values from 0.5 to 4
Outputs:
- factors: float32 [32, 1024, 1024], P(('grp', 'tm')), parts along dimension 0
The draws below stay inside these ranges and needn't reach their ends.
There are 2 independent parts, one for each index of `grp`. The reference program is written for one: setup_inputs(seed, part) draws one part's arguments, and reference() takes and returns one part's arrays. A program takes and returns all parts, laid end to end along the dimension named above; each array names one. Nothing has to cross between parts.
Inputs may be any that keep to these rules, and one draw needn't show every extreme that they name: `counts`: some step has exactly 2048 live rows in every draw.
All inputs are finite; a program needn't handle non-finite values. No bound on the sum of `counts` on one device may be relied on, other than what follows from the above.
Results may differ from the reference program's by a relative error of at most 0.0003.
Values sent between devices are 32-bit elements; how exact they have to be, the bound alone decides.
No kernel may reach another device: no remote copies, remote signals or barrier semaphores. Data moves between devices by JAX's collectives and lax.ppermute only.
A program may use at most 64 MiB of HBM per device.

```python
import math
import jax
import jax.numpy as jnp
import numpy as np
from jax import lax

S = 1024
CAP = 2048
STEPS = 16


def level_of(rng, shape, split, low, top_value):
    level = 1.0
    for dim, shards_of in split:
        steps = jax.random.uniform(jax.random.fold_in(jax.random.fold_in(rng, 6), dim), (shards_of,), jnp.float32, low / len(split), top_value / len(split))
        level = level * jnp.repeat(jnp.exp(steps), shape[dim] // shards_of).reshape((-1,) + (1,) * (len(shape) - 1 - dim))
    return level


def profile(number_of, total, reach, slope):
    weights = [(1 << 20) // math.isqrt(rank ** slope) + 1 for rank in range(2, number_of + 1)]
    rest, given = total - reach - (number_of - 1), [1] * (number_of - 1)
    while rest > 0:
        free = [i for i in range(number_of - 1) if given[i] < reach]
        mass, budget = sum([weights[i] for i in free]), rest
        for i in free:
            more = min(reach - given[i], max(1, budget * weights[i] // mass), rest)
            given[i] = given[i] + more
            rest = rest - more
    return np.array([reach] + given)


def uneven_parts(own_key, number_of, total, reach, lean):
    if number_of == 2:
        one = jax.random.randint(own_key, (), max(1, total - reach), min(reach, total - 1) + 1)
        return jnp.stack([one, total - one])
    sizes = jnp.asarray(profile(number_of, total, reach, lean), jnp.int32)
    twos = (number_of - 1) // 2
    donor, sink = sizes[1:1 + 2 * twos:2], sizes[2:2 + 2 * twos:2]
    slack = jnp.minimum(donor - 1, reach - sink)
    passed = jax.random.randint(jax.random.fold_in(own_key, 1), (twos,), 0, 1 << 20) % (slack + 1)
    sizes = sizes.at[1:1 + 2 * twos:2].set(donor - passed).at[2:2 + 2 * twos:2].set(sink + passed)
    return sizes[jax.random.permutation(jax.random.fold_in(own_key, 2), number_of)]


def scatter_about(rng, dims, width, reach, split=(), kind=jnp.bfloat16):
    result = width * jax.random.normal(rng, dims, jnp.float32)
    if split:
        result = result * level_of(rng, dims, split, -0.22, 0.18)
    return jnp.clip(result, -reach, reach).astype(kind)


def setup_inputs(seed: int = 0, part: int = 0) -> dict:
    seeds = jax.random.split(jax.random.key(seed), 4)
    own_keys = jax.random.split(jax.random.fold_in(seeds[3], part), 4)
    return {
        "observations": scatter_about(own_keys[0], (STEPS * CAP, S), S ** -0.5, 0.1875, ((0, 16),)),
        "counts": uneven_parts(own_keys[1], STEPS, STEPS * CAP // 3, CAP, 2).astype(jnp.int32),
        "prior": jnp.clip(jnp.exp(math.log(4.0) - 2.0794415 * jax.random.uniform(own_keys[2], (STEPS, S), jnp.float32) ** level_of(own_keys[2], (STEPS, S), ((0, 16),), -0.2, 0.2)), 0.5, 4.0),
    }


def masked_gram(observed, live_count, prior_step):
    capacity = observed.shape[0]
    row_index = jnp.arange(capacity, dtype=jnp.int32)
    widened = jnp.where((row_index < live_count)[:, None], observed.astype(jnp.float32), jnp.float32(0.0))
    gram_matrix = jnp.dot(widened.T.astype(jnp.float32), widened.astype(jnp.float32), precision=lax.Precision.HIGHEST, preferred_element_type=jnp.float32)
    return gram_matrix + jnp.diag(prior_step)

def reference(observations, counts, prior):
    stacked = observations.reshape(STEPS, CAP, S)
    grams = lax.map(lambda item: masked_gram(item[0], item[1], item[2]), (stacked, counts, prior))
    zeroed = jnp.zeros_like(grams)
    level_one = grams + jnp.concatenate([zeroed[:1], grams[:-1]], 0)
    level_two = level_one + jnp.concatenate([zeroed[:2], level_one[:-2]], 0)
    lower_factor = jnp.linalg.cholesky(level_two)
    return jnp.transpose(lower_factor, (0, 2, 1))
```

```python
import functools
import jax
import jax.numpy as jnp
from jax import lax
from jax.experimental import pallas as pl
from jax.experimental.pallas import tpu as pltpu
from jax.sharding import PartitionSpec as P

LANES = 128
SUBS = 8
MICRO = 32
ROWS = 256
DEPTH = 512
FULL = lax.Precision.HIGHEST


def dot_tn(a, b):
    return lax.dot_general(a, b, (((0,), (0,)), ((), ())), precision=FULL, preferred_element_type=jnp.float32)


def dot_nn(a, b):
    return lax.dot_general(a, b, (((1,), (0,)), ((), ())), precision=FULL, preferred_element_type=jnp.float32)


def row_of(x, i):
    return jnp.broadcast_to(x[i:i + 1, :], x.shape)


def lane_of(x, j):
    return jnp.broadcast_to(x[:, j:j + 1], x.shape)


def eliminate(tiles, first):
    sub = lax.broadcasted_iota(jnp.int32, (SUBS, LANES), 0)
    groups = len(tiles)
    for p in range(groups):
        cols = [[lane_of(tiles[g][0], first + SUBS * p + j) for g in range(p, groups)] for j in range(SUBS)]
        scale = None
        for i in range(SUBS):
            pivot = row_of(cols[i][0], i)
            inv = 1.0 / pivot
            root = lax.rsqrt(pivot)
            scale = root if scale is None else jnp.where(sub == i, root, scale)
            mult = [c * inv for c in cols[i]]
            mult[0] = jnp.where(sub > i, mult[0], 0.0)
            for j in range(i + 1, SUBS):
                e = row_of(cols[j][0], i)
                cols[j] = [c - m * e for c, m in zip(cols[j], mult)]
            for t in range(len(tiles[p])):
                e = row_of(tiles[p][t], i)
                for g in range(p, groups):
                    tiles[g][t] = tiles[g][t] - mult[g - p] * e
        tiles[p] = [t * scale for t in tiles[p]]
    return tiles


def factor_diag(d_ref):
    n = d_ref.shape[0]
    for r0 in range(0, n, MICRO):
        tiles = [[d_ref[r0 + SUBS * g:r0 + SUBS * (g + 1), LANES * t:LANES * (t + 1)] for t in range(2)] for g in range(MICRO // SUBS)]
        tiles = eliminate(tiles, r0)
        for g, row in enumerate(tiles):
            for t, tile in enumerate(row):
                d_ref[r0 + SUBS * g:r0 + SUBS * (g + 1), LANES * t:LANES * (t + 1)] = tile
        r1 = r0 + MICRO
        if r1 < n:
            u = d_ref[r0:r1, :]
            d_ref[r1:, :] = d_ref[r1:, :] - dot_tn(u[:, :LANES], u)[r1:]


def chunk_kernel(start, n_parts, *refs):
    parts = refs[:n_parts]
    refs = refs[n_parts:]
    if start:
        prev_ref, out_ref, a_ref, d_ref, o_ref, u_ref, sem = refs
    else:
        out_ref, a_ref, d_ref, o_ref, sem = refs
    rows, width = a_ref.shape
    size = start + width
    if start:
        fetch = pltpu.make_async_copy(prev_ref.at[pl.ds(0, start), pl.ds(start, width)], u_ref, sem.at[0])
        fetch.start()
    total = parts[0][...]
    for p in parts[1:]:
        total = total + p[...]
    if start:
        fetch.wait()
        total = total - dot_tn(u_ref[:, :rows], u_ref[...])
    a_ref[...] = total
    o_ref[...] = jnp.zeros_like(o_ref)
    r = lax.broadcasted_iota(jnp.int32, (LANES, LANES), 0)
    c = lax.broadcasted_iota(jnp.int32, (LANES, LANES), 1)
    eye = jnp.where(r == c, 1.0, 0.0).astype(jnp.float32)
    for b in range(0, rows, LANES):
        e = b + LANES
        d_ref[:, :LANES] = a_ref[b:e, b:e]
        d_ref[:, LANES:] = eye
        factor_diag(d_ref)
        o_ref[b:e, start + b:start + e] = jnp.where(r <= c, d_ref[:, :LANES], 0.0)
        if e < width:
            u = dot_nn(d_ref[:, LANES:], a_ref[b:e, e:])
            o_ref[b:e, start + e:] = u
            if e < rows:
                a_ref[e:, e:] = a_ref[e:, e:] - dot_tn(u[:, :rows - e], u)
    put = pltpu.make_async_copy(o_ref, out_ref.at[pl.ds(start, rows), :], sem.at[1])
    put.start()
    put.wait()


def factor_rows(start, rows, size, parts, prev):
    width = size - start
    f32 = jnp.float32
    scratch = [pltpu.VMEM((rows, width), f32), pltpu.VMEM((LANES, 2 * LANES), f32), pltpu.VMEM((rows, size), f32)]
    in_specs = [pl.BlockSpec(memory_space=pltpu.VMEM)] * len(parts)
    args = list(parts)
    aliases = {}
    if start:
        in_specs.append(pl.BlockSpec(memory_space=pl.ANY))
        args.append(prev)
        aliases = {len(parts): 0}
        scratch.append(pltpu.VMEM((start, width), f32))
    scratch.append(pltpu.SemaphoreType.DMA((2,)))
    return pl.pallas_call(
        functools.partial(chunk_kernel, start, len(parts)),
        out_shape=jax.ShapeDtypeStruct((size, size), f32),
        in_specs=in_specs,
        out_specs=pl.BlockSpec(memory_space=pl.ANY),
        scratch_shapes=scratch,
        input_output_aliases=aliases,
        name=f"factor_{start}",
    )(*args)


def gram_kernel(count_ref, h_ref, prior_ref, out_ref):
    k = pl.program_id(0)
    depth = h_ref.shape[0]
    rows, width = out_ref.shape
    start = h_ref.shape[1] - width
    left = count_ref[0] - k * depth

    @pl.when(k == 0)
    def _():
        r = lax.broadcasted_iota(jnp.int32, (rows, rows), 0)
        c = lax.broadcasted_iota(jnp.int32, (rows, rows), 1)
        out_ref[:, :rows] = jnp.where(r == c, jnp.broadcast_to(prior_ref[:, start:start + rows], (rows, rows)), 0.0)
        if width > rows:
            out_ref[:, rows:] = jnp.zeros((rows, width - rows), jnp.float32)

    @pl.when(left > 0)
    def _():
        index = lax.broadcasted_iota(jnp.int32, h_ref.shape, 0)
        h = jnp.where(index < left, h_ref[...], jnp.zeros_like(h_ref))[:, start:]
        out_ref[...] += lax.dot_general(h[:, :rows], h, (((0,), (0,)), ((), ())), preferred_element_type=jnp.float32)


def gram_rows(start, rows, observations, counts, prior):
    capacity, size = observations.shape
    depth = min(DEPTH, capacity)
    width = size - start

    def block(k, count):
        return jnp.minimum(k, (count[0] - 1) // depth), 0

    grid_spec = pltpu.PrefetchScalarGridSpec(
        num_scalar_prefetch=1,
        grid=(capacity // depth,),
        in_specs=[
            pl.BlockSpec((depth, size), block),
            pl.BlockSpec((1, size), lambda k, count: (0, 0)),
        ],
        out_specs=pl.BlockSpec((rows, width), lambda k, count: (0, 0)),
    )
    return pl.pallas_call(
        gram_kernel,
        out_shape=jax.ShapeDtypeStruct((rows, width), jnp.float32),
        grid_spec=grid_spec,
        name=f"gram_{start}",
    )(counts, observations, prior)


def from_behind(block, axis, distance):
    devices = range(lax.axis_size(axis))
    route = [(i - distance, i) for i in devices if i - distance in devices]
    return lax.ppermute(block, axis, route)


def body(observations, counts, prior):
    size = observations.shape[1]
    starts = range(0, size, ROWS)
    parts = []
    for start in starts:
        gram = gram_rows(start, ROWS, observations, counts, prior)
        level_one = gram + from_behind(gram, "tm", 1)
        parts.append([level_one, from_behind(level_one, "tm", 2)])
    factor = None
    for start, part in zip(starts, parts):
        factor = factor_rows(start, ROWS, size, part, factor)
    return factor[None]


def solution(mesh):
    placed = (P(("grp", "tm"), None), P(("grp", "tm")), P(("grp", "tm"), None))
    return jax.shard_map(
        body, mesh=mesh, in_specs=placed, out_specs=P(("grp", "tm"), None, None), check_vma=False
    )
```

```python
import functools
import jax
import jax.numpy as jnp
from jax import lax
from jax.experimental import pallas as pl
from jax.experimental.pallas import tpu as pltpu
from jax.sharding import PartitionSpec as P


LANES = 128
SUBS = 8
MICRO = 32
DEPTH = 512
CUTS = (1, 3, 5)
FULL = lax.Precision.HIGHEST


def dot_tn(a, b):
    return lax.dot_general(a, b, (((0,), (0,)), ((), ())), precision=FULL, preferred_element_type=jnp.float32)


def dot_nn(a, b):
    return lax.dot_general(a, b, (((1,), (0,)), ((), ())), precision=FULL, preferred_element_type=jnp.float32)


def row_of(x, i):
    return jnp.broadcast_to(x[i:i + 1, :], x.shape)


def lane_of(x, j):
    return jnp.broadcast_to(x[:, j:j + 1], x.shape)


def eliminate(tiles, first):
    sub = lax.broadcasted_iota(jnp.int32, (SUBS, LANES), 0)
    groups = len(tiles)
    for p in range(groups):
        cols = [[lane_of(tiles[g][0], first + SUBS * p + j) for g in range(p, groups)] for j in range(SUBS)]
        scale = None
        for i in range(SUBS):
            pivot = row_of(cols[i][0], i)
            inv = 1.0 / pivot
            root = lax.rsqrt(pivot)
            scale = root if scale is None else jnp.where(sub == i, root, scale)
            mult = [c * inv for c in cols[i]]
            mult[0] = jnp.where(sub > i, mult[0], 0.0)
            for j in range(i + 1, SUBS):
                e = row_of(cols[j][0], i)
                cols[j] = [c - m * e for c, m in zip(cols[j], mult)]
            for t in range(len(tiles[p])):
                e = row_of(tiles[p][t], i)
                for g in range(p, groups):
                    tiles[g][t] = tiles[g][t] - mult[g - p] * e
        tiles[p] = [t * scale for t in tiles[p]]
    return tiles


def factor_diag(d_ref):
    n = d_ref.shape[0]
    for r0 in range(0, n, MICRO):
        tiles = [[d_ref[r0 + SUBS * g:r0 + SUBS * (g + 1), LANES * t:LANES * (t + 1)] for t in range(2)] for g in range(MICRO // SUBS)]
        tiles = eliminate(tiles, r0)
        for g, row in enumerate(tiles):
            for t, tile in enumerate(row):
                d_ref[r0 + SUBS * g:r0 + SUBS * (g + 1), LANES * t:LANES * (t + 1)] = tile
        r1 = r0 + MICRO
        if r1 < n:
            u = d_ref[r0:r1, :]
            d_ref[r1:, :] = d_ref[r1:, :] - dot_tn(u[:, :LANES], u)[r1:]


def groups_of(size):
    edges = [0, *[c for c in CUTS if c * LANES < size], size // LANES]
    return list(zip(edges[:-1], edges[1:]))


def panels(group, size):
    at, out = 0, []
    for r in range(*group):
        width = size - r * LANES
        out.append((r, at, width))
        at += width
    return out, at


def gram_kernel(groups, count_ref, h_ref, prior_ref, *out_refs):
    k = pl.program_id(0)
    depth, size = h_ref.shape
    left = count_ref[0] - k * depth

    @pl.when(k == 0)
    def _():
        r = lax.broadcasted_iota(jnp.int32, (LANES, LANES), 0)
        c = lax.broadcasted_iota(jnp.int32, (LANES, LANES), 1)
        for group, out_ref in zip(groups, out_refs):
            out_ref[...] = jnp.zeros_like(out_ref)
            for b, at, _ in panels(group, size)[0]:
                diag = jnp.broadcast_to(prior_ref[:, b * LANES:(b + 1) * LANES], (LANES, LANES))
                out_ref[:, at:at + LANES] = jnp.where(r == c, diag, 0.0)

    @pl.when(left > 0)
    def _():
        index = lax.broadcasted_iota(jnp.int32, h_ref.shape, 0)
        h = jnp.where(index < left, h_ref[...], jnp.zeros_like(h_ref))
        for group, out_ref in zip(groups, out_refs):
            first, last = group[0] * LANES, group[1] * LANES
            gram = lax.dot_general(h[:, first:last], h[:, first:], (((0,), (0,)), ((), ())), preferred_element_type=jnp.float32)
            for b, at, width in panels(group, size)[0]:
                r = b * LANES - first
                out_ref[:, at:at + width] += gram[r:r + LANES, r:]


def gram_rows(groups, observations, counts, prior):
    capacity, size = observations.shape
    depth = min(DEPTH, capacity)
    totals = [panels(group, size)[1] for group in groups]

    def block(k, count):
        return jnp.minimum(k, (count[0] - 1) // depth), 0

    grid_spec = pltpu.PrefetchScalarGridSpec(
        num_scalar_prefetch=1,
        grid=(capacity // depth,),
        in_specs=[pl.BlockSpec((depth, size), block), pl.BlockSpec((1, size), lambda k, count: (0, 0))],
        out_specs=[pl.BlockSpec((LANES, total), lambda k, count: (0, 0)) for total in totals],
    )
    return pl.pallas_call(
        functools.partial(gram_kernel, groups),
        out_shape=[jax.ShapeDtypeStruct((LANES, total), jnp.float32) for total in totals],
        grid_spec=grid_spec,
    )(counts, observations, prior)


def factor_kernel(group, odd_ref, own_ref, pair_ref, far_ref, near_ref, *refs):
    start = group[0] * LANES
    if start:
        prev_ref, out_ref, d_ref, o_ref, u_ref, sem = refs
    else:
        out_ref, d_ref, o_ref, sem = refs
    rows, size = o_ref.shape
    if start:
        fetch = pltpu.make_async_copy(prev_ref.at[pl.ds(0, start), pl.ds(start, size - start)], u_ref, sem.at[0])
        fetch.start()
    odd = odd_ref[0] > 0
    total = own_ref[...] + far_ref[...] + near_ref[...] + jnp.where(odd, pair_ref[...], 0.0)
    o_ref[...] = jnp.zeros_like(o_ref)
    r = lax.broadcasted_iota(jnp.int32, (LANES, LANES), 0)
    c = lax.broadcasted_iota(jnp.int32, (LANES, LANES), 1)
    eye = jnp.where(r == c, 1.0, 0.0).astype(jnp.float32)
    if start:
        fetch.wait()
    for b, at, width in panels(group, size)[0]:
        a = total[:, at:at + width]
        s = b * LANES
        if start:
            u = u_ref[:, s - start:]
            a = a - dot_tn(u[:, :LANES], u)
        if s > start:
            u = o_ref[:s - start, s:]
            a = a - dot_tn(u[:, :LANES], u)
        d_ref[:, :LANES] = a[:, :LANES]
        d_ref[:, LANES:] = eye
        factor_diag(d_ref)
        o_ref[s - start:s - start + LANES, s:s + LANES] = jnp.where(r <= c, d_ref[:, :LANES], 0.0)
        if width > LANES:
            o_ref[s - start:s - start + LANES, s + LANES:] = dot_nn(d_ref[:, LANES:], a[:, LANES:])
    put = pltpu.make_async_copy(o_ref, out_ref.at[pl.ds(start, rows), :], sem.at[1])
    put.start()
    put.wait()


def factor_rows(group, size, odd, parts, prev):
    start, rows = group[0] * LANES, (group[1] - group[0]) * LANES
    f32 = jnp.float32
    scratch = [pltpu.VMEM((LANES, 2 * LANES), f32), pltpu.VMEM((rows, size), f32)]
    in_specs = [pl.BlockSpec(memory_space=pltpu.SMEM)] + [pl.BlockSpec(memory_space=pltpu.VMEM)] * len(parts)
    args = [odd, *parts]
    aliases = {}
    if start:
        aliases = {len(args): 0}
        in_specs.append(pl.BlockSpec(memory_space=pl.ANY))
        args.append(prev)
        scratch.append(pltpu.VMEM((start, size - start), f32))
    scratch.append(pltpu.SemaphoreType.DMA((2,)))
    return pl.pallas_call(
        functools.partial(factor_kernel, group),
        out_shape=jax.ShapeDtypeStruct((size, size), f32),
        in_specs=in_specs,
        out_specs=pl.BlockSpec(memory_space=pl.ANY),
        scratch_shapes=scratch,
        input_output_aliases=aliases,
    )(*args)


def body(observations, counts, prior):
    size = observations.shape[1]
    steps = lax.axis_size("tm")
    groups = groups_of(size)
    odd = lax.rem(lax.axis_index("tm"), 2)
    swap = [(t, t ^ 1) for t in range(steps)]
    ahead = [(t, t + 3) for t in range(steps - 3)]
    inward = [(t, t - 1) for t in range(1, steps, 2)]
    owns = []
    for share in (groups[:1], groups[1:2], groups[2:]):
        owns += gram_rows(share, observations, counts, prior)
    parts = []
    for own in owns:
        pair = lax.ppermute(own, "tm", swap)
        send = jnp.where(odd == 0, own + pair, own)
        far = lax.ppermute(send, "tm", ahead)
        near = lax.ppermute(far, "tm", inward)
        parts.append([own, pair, far, near])
    factor = None
    for group, part in zip(groups, parts):
        factor = factor_rows(group, size, odd[None], part, factor)
    return factor[None]


def solution(mesh):
    placed = (P(("grp", "tm"), None), P(("grp", "tm")), P(("grp", "tm"), None))
    return jax.shard_map(
        body, mesh=mesh, in_specs=placed, out_specs=P(("grp", "tm"), None, None), check_vma=False
    )
```

```python
import functools
import jax
import jax.numpy as jnp
from jax import lax
from jax.experimental import pallas as pl
from jax.experimental.pallas import tpu as pltpu
from jax.sharding import PartitionSpec as P


LANES = 128
SUBS = 8
MICRO = 32
DEPTH = 512
ROOM = 24 << 20
CUTS = (1, 2, 4)


def parts_of(x):
    out = []
    for _ in range(3):
        out.append(x.astype(jnp.bfloat16))
        x = x - out[-1].astype(jnp.float32)
    return out


def exact_tn(a, b):
    a, b = parts_of(a), parts_of(b)
    order = ((0, 0), (0, 1), (1, 0), (1, 1), (0, 2), (2, 0))
    left = jnp.concatenate([a[i] for i, _ in order], 0)
    right = jnp.concatenate([b[j] for _, j in order], 0)
    return lax.dot_general(left, right, (((0,), (0,)), ((), ())), preferred_element_type=jnp.float32)


def exact_nn(a, b):
    a, b = parts_of(a), parts_of(b)
    order = ((0, 0), (0, 1), (1, 0), (1, 1), (0, 2), (2, 0))
    left = jnp.concatenate([a[i] for i, _ in order], 1)
    right = jnp.concatenate([b[j] for _, j in order], 0)
    return lax.dot_general(left, right, (((1,), (0,)), ((), ())), preferred_element_type=jnp.float32)


def row_of(x, i):
    return jnp.broadcast_to(x[i:i + 1, :], x.shape)


def lane_of(x, j):
    return jnp.take_along_axis(x, jnp.full(x.shape, j, jnp.int32), axis=1)


def eliminate(tiles, first):
    sub = lax.broadcasted_iota(jnp.int32, (SUBS, LANES), 0)
    groups = len(tiles)
    for p in range(groups):
        cols = [[lane_of(tiles[g][0], first + SUBS * p + j) for g in range(p, groups)] for j in range(SUBS)]
        scale, mix = None, None
        for i in range(0, SUBS, 2):
            x, y = cols[i], cols[i + 1]
            aa, ab, bb = row_of(x[0], i), row_of(y[0], i), row_of(y[0], i + 1)
            det = aa * bb - ab * ab
            ra, rd = 1.0 / aa, 1.0 / det
            root = lax.rsqrt(aa)
            tail = aa * root * lax.rsqrt(det)
            skew = ab * ra
            scale = jnp.where(sub == i + 1, tail, root if scale is None else jnp.where(sub == i, root, scale))
            mix = jnp.where(sub == i + 1, skew, 0.0 if mix is None else mix)
            w = [v * aa - u * ab for u, v in zip(x, y)]
            x = [jnp.where(sub > i + 1, x[0], 0.0), *x[1:]]
            w[0] = jnp.where(sub > i + 1, w[0], 0.0)
            mx, mw = [v * ra for v in x], [v * rd for v in w]
            for j in range(i + 2, SUBS):
                e, f = row_of(cols[j][0], i), row_of(cols[j][0], i + 1)
                h = f * aa - e * ab
                if j < i + 4:
                    cols[j] = [(c - (u * e) * ra) - ((v * h) * ra) * rd for c, u, v in zip(cols[j], x, w)]
                else:
                    h = h * ra
                    cols[j] = [c - u * e - v * h for c, u, v in zip(cols[j], mx, mw)]
            for t in range(len(tiles[p])):
                e, f = row_of(tiles[p][t], i), row_of(tiles[p][t], i + 1)
                h = f - skew * e
                for g in range(p, groups):
                    tiles[g][t] = tiles[g][t] - mx[g - p] * e - mw[g - p] * h
        for t in range(len(tiles[p])):
            v = tiles[p][t]
            tiles[p][t] = (v - mix * pltpu.roll(v, 1, 0)) * scale
    return tiles


def factor_diag(d_ref):
    n = d_ref.shape[0]
    for r0 in range(0, n, MICRO):
        tiles = [[d_ref[r0 + SUBS * g:r0 + SUBS * (g + 1), LANES * t:LANES * (t + 1)] for t in range(2)] for g in range(MICRO // SUBS)]
        tiles = eliminate(tiles, r0)
        for g, row in enumerate(tiles):
            for t, tile in enumerate(row):
                d_ref[r0 + SUBS * g:r0 + SUBS * (g + 1), LANES * t:LANES * (t + 1)] = tile
        r1 = r0 + MICRO
        if r1 < n:
            u = d_ref[r0:r1, :]
            d_ref[r1:, :] = d_ref[r1:, :] - exact_tn(u[:, :LANES], u)[r1:]


def groups_of(size):
    edges = [0, *[c for c in CUTS if c * LANES < size], size // LANES]
    return list(zip(edges[:-1], edges[1:]))


def panels(group, size):
    at, out = 0, []
    for r in range(*group):
        width = size - r * LANES
        out.append((r, at, width))
        at += width
    return out, at


def gram_kernel(groups, count_ref, h_ref, prior_ref, *out_refs):
    k = pl.program_id(0)
    depth, size = h_ref.shape
    left = count_ref[0] - k * depth

    @pl.when(k == 0)
    def _():
        r = lax.broadcasted_iota(jnp.int32, (LANES, LANES), 0)
        c = lax.broadcasted_iota(jnp.int32, (LANES, LANES), 1)
        for group, out_ref in zip(groups, out_refs):
            out_ref[...] = jnp.zeros_like(out_ref)
            for b, at, _ in panels(group, size)[0]:
                diag = jnp.broadcast_to(prior_ref[:, b * LANES:(b + 1) * LANES], (LANES, LANES))
                out_ref[:, at:at + LANES] = jnp.where(r == c, diag, 0.0)

    def add(h):
        for group, out_ref in zip(groups, out_refs):
            first, last = group[0] * LANES, group[1] * LANES
            gram = lax.dot_general(h[:, first:last], h[:, first:], (((0,), (0,)), ((), ())), preferred_element_type=jnp.float32)
            for b, at, width in panels(group, size)[0]:
                r = b * LANES - first
                out_ref[:, at:at + width] += gram[r:r + LANES, r:]

    @pl.when(left >= depth)
    def _():
        add(h_ref[...])

    @pl.when(jnp.logical_and(left > 0, left < depth))
    def _():
        index = lax.broadcasted_iota(jnp.int32, h_ref.shape, 0)
        add(jnp.where(index < left, h_ref[...], jnp.zeros_like(h_ref)))


def gram_rows(groups, observations, counts, prior):
    capacity, size = observations.shape
    depth = min(DEPTH, capacity)
    totals = [panels(group, size)[1] for group in groups]

    def block(k, count):
        return jnp.minimum(k, (count[0] - 1) // depth), 0

    grid_spec = pltpu.PrefetchScalarGridSpec(
        num_scalar_prefetch=1,
        grid=(capacity // depth,),
        in_specs=[pl.BlockSpec((depth, size), block), pl.BlockSpec((1, size), lambda k, count: (0, 0))],
        out_specs=[pl.BlockSpec((LANES, total), lambda k, count: (0, 0)) for total in totals],
    )
    return pl.pallas_call(
        functools.partial(gram_kernel, groups),
        out_shape=[jax.ShapeDtypeStruct((LANES, total), jnp.float32) for total in totals],
        grid_spec=grid_spec,
        compiler_params=pltpu.CompilerParams(vmem_limit_bytes=ROOM),
    )(counts, observations, prior)


def factor_kernel(group, odd_ref, own_ref, pair_ref, far_ref, near_ref, *refs):
    start = group[0] * LANES
    if start:
        prev_ref, out_ref, d_ref, o_ref, u_ref, sem = refs
    else:
        out_ref, d_ref, o_ref, sem = refs
    rows, size = o_ref.shape
    if start:
        fetch = pltpu.make_async_copy(prev_ref.at[pl.ds(0, start), pl.ds(start, size - start)], u_ref, sem.at[0])
        fetch.start()
    odd = odd_ref[0] > 0
    total = own_ref[...] + far_ref[...] + near_ref[...] + jnp.where(odd, pair_ref[...], 0.0)
    o_ref[...] = jnp.zeros_like(o_ref)
    r = lax.broadcasted_iota(jnp.int32, (LANES, LANES), 0)
    c = lax.broadcasted_iota(jnp.int32, (LANES, LANES), 1)
    eye = jnp.where(r == c, 1.0, 0.0).astype(jnp.float32)
    if start:
        fetch.wait()
    for b, at, width in panels(group, size)[0]:
        a = total[:, at:at + width]
        s = b * LANES
        if start:
            u = u_ref[:, s - start:]
            a = a - exact_tn(u[:, :LANES], u)
        if s > start:
            u = o_ref[:s - start, s:]
            a = a - exact_tn(u[:, :LANES], u)
        d_ref[:, :LANES] = a[:, :LANES]
        d_ref[:, LANES:] = eye
        factor_diag(d_ref)
        o_ref[s - start:s - start + LANES, s:s + LANES] = jnp.where(r <= c, d_ref[:, :LANES], 0.0)
        if width > LANES:
            o_ref[s - start:s - start + LANES, s + LANES:] = exact_nn(d_ref[:, LANES:], a[:, LANES:])
    put = pltpu.make_async_copy(o_ref, out_ref.at[pl.ds(start, rows), :], sem.at[1])
    put.start()
    put.wait()


def factor_rows(group, size, odd, parts, prev):
    start, rows = group[0] * LANES, (group[1] - group[0]) * LANES
    f32 = jnp.float32
    scratch = [pltpu.VMEM((LANES, 2 * LANES), f32), pltpu.VMEM((rows, size), f32)]
    in_specs = [pl.BlockSpec(memory_space=pltpu.SMEM)] + [pl.BlockSpec(memory_space=pltpu.VMEM)] * len(parts)
    args = [odd, *parts]
    aliases = {}
    if start:
        aliases = {len(args): 0}
        in_specs.append(pl.BlockSpec(memory_space=pl.ANY))
        args.append(prev)
        scratch.append(pltpu.VMEM((start, size - start), f32))
    scratch.append(pltpu.SemaphoreType.DMA((2,)))
    return pl.pallas_call(
        functools.partial(factor_kernel, group),
        out_shape=jax.ShapeDtypeStruct((size, size), f32),
        in_specs=in_specs,
        out_specs=pl.BlockSpec(memory_space=pl.ANY),
        scratch_shapes=scratch,
        input_output_aliases=aliases,
        compiler_params=pltpu.CompilerParams(vmem_limit_bytes=ROOM),
    )(*args)


def body(observations, counts, prior):
    size = observations.shape[1]
    steps = lax.axis_size("tm")
    groups = groups_of(size)
    odd = lax.rem(lax.axis_index("tm"), 2)
    swap = [(t, t ^ 1) for t in range(steps)]
    ahead = [(t, t + 3) for t in range(steps - 3)]
    inward = [(t, t - 1) for t in range(1, steps, 2)]
    owns = []
    for share in (groups[:1], groups[1:]):
        owns += gram_rows(share, observations, counts, prior)
    parts = []
    for own in owns:
        pair = lax.ppermute(own, "tm", swap)
        send = jnp.where(odd == 0, own + pair, own)
        far = lax.ppermute(send, "tm", ahead)
        near = lax.ppermute(far, "tm", inward)
        parts.append([own, pair, far, near])
    factor = None
    for group, part in zip(groups, parts):
        factor = factor_rows(group, size, odd[None], part, factor)
    return factor[None]


def solution(mesh):
    placed = (P(("grp", "tm"), None), P(("grp", "tm")), P(("grp", "tm"), None))
    return jax.shard_map(
        body, mesh=mesh, in_specs=placed, out_specs=P(("grp", "tm"), None, None), check_vma=False
    )
```

```python
import functools
import jax
import jax.numpy as jnp
from jax import lax
from jax.experimental import pallas as pl
from jax.experimental.pallas import tpu as pltpu
from jax.sharding import PartitionSpec as P


LANES = 128
SUBS = 8
MICRO = 32
DEPTH = 512
ROOM = 24 << 20
CUTS = (1, 2, 4)
SETTLE = 2


def parts_of(x):
    out = []
    for _ in range(3):
        out.append(x.astype(jnp.bfloat16))
        x = x - out[-1].astype(jnp.float32)
    return out


def exact_tn(a, b):
    a, b = parts_of(a), parts_of(b)
    order = ((0, 0), (0, 1), (1, 0), (1, 1), (0, 2), (2, 0))
    left = jnp.concatenate([a[i] for i, _ in order], 0)
    right = jnp.concatenate([b[j] for _, j in order], 0)
    return lax.dot_general(left, right, (((0,), (0,)), ((), ())), preferred_element_type=jnp.float32)


def exact_nn(a, b):
    a, b = parts_of(a), parts_of(b)
    order = ((0, 0), (0, 1), (1, 0), (1, 1), (0, 2), (2, 0))
    left = jnp.concatenate([a[i] for i, _ in order], 1)
    right = jnp.concatenate([b[j] for _, j in order], 0)
    return lax.dot_general(left, right, (((1,), (0,)), ((), ())), preferred_element_type=jnp.float32)


def row_of(x, i):
    return jnp.broadcast_to(x[i:i + 1, :], x.shape)


def lane_of(x, j):
    return jnp.take_along_axis(x, jnp.full(x.shape, j, jnp.int32), axis=1)


def eliminate(tiles, first):
    sub = lax.broadcasted_iota(jnp.int32, (SUBS, LANES), 0)
    groups = len(tiles)
    for p in range(groups):
        cols = [[lane_of(tiles[g][0], first + SUBS * p + j) for g in range(p, groups)] for j in range(SUBS)]
        scale, mix = None, None
        for i in range(0, SUBS, 2):
            x, y = cols[i], cols[i + 1]
            aa, ab, bb = row_of(x[0], i), row_of(y[0], i), row_of(y[0], i + 1)
            det = aa * bb - ab * ab
            ra, rd = 1.0 / aa, 1.0 / det
            root = lax.rsqrt(aa)
            tail = aa * root * lax.rsqrt(det)
            skew = ab * ra
            scale = jnp.where(sub == i + 1, tail, root if scale is None else jnp.where(sub == i, root, scale))
            mix = jnp.where(sub == i + 1, skew, 0.0 if mix is None else mix)
            w = jnp.where(sub > i + 1, y[0] * aa - x[0] * ab, 0.0)
            z = jnp.where(sub > i + 1, x[0], 0.0)
            mx = [u * ra for u in (z, *x[1:])]
            mw = [w * rd, *((v - m * ab) * (aa * rd) for v, m in zip(y[1:], mx[1:]))]
            for j in range(i + 2, SUBS):
                own, *rest = cols[j]
                e, f = row_of(own, i), row_of(own, i + 1)
                h = f - skew * e
                if j < i + 4:
                    own = (own - (z * e) * ra) - ((w * (f * aa - e * ab)) * ra) * rd
                else:
                    own = own - mx[0] * e - mw[0] * h
                cols[j] = [own, *(c - u * e - v * h for c, u, v in zip(rest, mx[1:], mw[1:]))]
            for t in range(len(tiles[p])):
                e, f = row_of(tiles[p][t], i), row_of(tiles[p][t], i + 1)
                h = f - skew * e
                for g in range(p, groups):
                    tiles[g][t] = tiles[g][t] - mx[g - p] * e - mw[g - p] * h
        for t in range(len(tiles[p])):
            v = tiles[p][t]
            tiles[p][t] = (v - mix * pltpu.roll(v, 1, 0)) * scale
    return tiles


def factor_diag(d_ref):
    n = d_ref.shape[0]
    for r0 in range(0, n, MICRO):
        tiles = [[d_ref[r0 + SUBS * g:r0 + SUBS * (g + 1), LANES * t:LANES * (t + 1)] for t in range(2)] for g in range(MICRO // SUBS)]
        tiles = eliminate(tiles, r0)
        for g, row in enumerate(tiles):
            for t, tile in enumerate(row):
                d_ref[r0 + SUBS * g:r0 + SUBS * (g + 1), LANES * t:LANES * (t + 1)] = tile
        r1 = r0 + MICRO
        if r1 < n:
            u = d_ref[r0:r1, :]
            d_ref[r1:, :] = d_ref[r1:, :] - exact_tn(u[:, :LANES], u)[r1:]


def groups_of(size):
    edges = [0, *[c for c in CUTS if c * LANES < size], size // LANES]
    return list(zip(edges[:-1], edges[1:]))


def panels(group, size):
    at, out = 0, []
    for r in range(*group):
        width = size - r * LANES
        out.append((r, at, width))
        at += width
    return out, at


def add_grams(groups, h, out_refs):
    size = h.shape[1]
    for group, out_ref in zip(groups, out_refs):
        first, last = group[0] * LANES, group[1] * LANES
        gram = lax.dot_general(h[:, first:last], h[:, first:], (((0,), (0,)), ((), ())), preferred_element_type=jnp.float32)
        for b, at, width in panels(group, size)[0]:
            r = b * LANES - first
            out_ref[:, at:at + width] += gram[r:r + LANES, r:]


def set_priors(groups, prior_ref, out_refs):
    size = prior_ref.shape[1]
    r = lax.broadcasted_iota(jnp.int32, (LANES, LANES), 0)
    c = lax.broadcasted_iota(jnp.int32, (LANES, LANES), 1)
    for group, out_ref in zip(groups, out_refs):
        out_ref[...] = jnp.zeros_like(out_ref)
        for b, at, _ in panels(group, size)[0]:
            diag = jnp.broadcast_to(prior_ref[:, b * LANES:(b + 1) * LANES], (LANES, LANES))
            out_ref[:, at:at + LANES] = jnp.where(r == c, diag, 0.0)


def live_rows(h, left):
    index = lax.broadcasted_iota(jnp.int32, h.shape, 0)
    return jnp.where(index < left, h, jnp.zeros_like(h))


def gram_kernel(groups, fetched, count_ref, h_ref, prior_ref, *refs):
    n = len(groups)
    out_refs, refs = refs[:n], refs[n:]
    depth = min(DEPTH, h_ref.shape[0])
    pieces = h_ref.shape[0] // depth
    rows_ref = h_ref
    if fetched:
        rows_ref, bias_ref, sem = refs
        bias = pltpu.make_async_copy(prior_ref, bias_ref, sem.at[pieces])
        bias.start()

    def fetch(k):
        rows = pl.ds(k * depth, depth)
        return pltpu.make_async_copy(h_ref.at[rows, :], rows_ref.at[rows, :], sem.at[k])

    if fetched:
        for k in range(pieces):
            pl.when(k * depth < count_ref[0])(fetch(k).start)
        bias.wait()
    set_priors(groups, bias_ref if fetched else prior_ref, out_refs)
    for k in range(pieces):
        left = count_ref[0] - k * depth
        rows = slice(k * depth, (k + 1) * depth)
        if fetched:
            pl.when(left > 0)(fetch(k).wait)

        @pl.when(left >= depth)
        def _():
            add_grams(groups, rows_ref[rows, :], out_refs)

        @pl.when(jnp.logical_and(left > 0, left < depth))
        def _():
            add_grams(groups, live_rows(rows_ref[rows, :], left), out_refs)


def gram_rows(groups, fetched, observations, counts, prior):
    capacity, size = observations.shape
    totals = [panels(group, size)[1] for group in groups]
    vmem, smem = pl.BlockSpec(memory_space=pltpu.VMEM), pl.BlockSpec(memory_space=pltpu.SMEM)
    if fetched:
        observations = pltpu.with_memory_space_constraint(observations, pltpu.HBM)
        prior = pltpu.with_memory_space_constraint(prior, pltpu.HBM)
        place = pl.BlockSpec(memory_space=pltpu.HBM)
        scratch = [
            pltpu.VMEM((capacity, size), observations.dtype),
            pltpu.VMEM((1, size), prior.dtype),
            pltpu.SemaphoreType.DMA((1 + max(1, capacity // DEPTH),)),
        ]
    else:
        place, scratch = vmem, []
    return pl.pallas_call(
        functools.partial(gram_kernel, groups, fetched),
        out_shape=[jax.ShapeDtypeStruct((LANES, total), jnp.float32) for total in totals],
        in_specs=[smem, place, place],
        out_specs=[vmem] * len(groups),
        scratch_shapes=scratch,
        compiler_params=pltpu.CompilerParams(vmem_limit_bytes=ROOM),
    )(counts, observations, prior)


def own_sum(odd_ref, own, pair):
    return own + jnp.where(odd_ref[0] > 0, pair, 0.0)


def settle_kernel(groups, odd_ref, *refs):
    n = len(groups)
    owns, pairs, (factor_ref, *outs), (u_ref, sem) = refs[:n], refs[n:2 * n], refs[2 * n:-2], refs[-2:]
    known, width = u_ref.shape
    size = known + width
    fetch = pltpu.make_async_copy(factor_ref.at[pl.ds(0, known), pl.ds(known, width)], u_ref, sem)
    fetch.start()
    fetch.wait()
    for group, own_ref, pair_ref, out_ref in zip(groups, owns, pairs, outs):
        for b, at, w in panels(group, size)[0]:
            s = b * LANES - known
            part = own_sum(odd_ref, own_ref[:, at:at + w], pair_ref[:, at:at + w])
            out_ref[:, at:at + w] = part - exact_tn(u_ref[:, s:s + LANES], u_ref[:, s:])


def settle_rows(groups, size, odd, owns, pairs, factor):
    vmem, smem, f32 = pl.BlockSpec(memory_space=pltpu.VMEM), pl.BlockSpec(memory_space=pltpu.SMEM), jnp.float32
    known = groups[0][0] * LANES
    return pl.pallas_call(
        functools.partial(settle_kernel, groups),
        out_shape=[jax.ShapeDtypeStruct(own.shape, f32) for own in owns],
        in_specs=[smem] + [vmem] * (2 * len(groups)) + [pl.BlockSpec(memory_space=pl.ANY)],
        out_specs=[vmem] * len(groups),
        scratch_shapes=[pltpu.VMEM((known, size - known), f32), pltpu.SemaphoreType.DMA],
        compiler_params=pltpu.CompilerParams(vmem_limit_bytes=ROOM),
        name="settle",
    )(odd, *owns, *pairs, factor)


def factor_kernel(group, known, n_parts, odd_ref, *refs):
    start = group[0] * LANES
    parts, refs = refs[:n_parts], refs[n_parts:]
    if start:
        prev_ref, refs = refs[0], refs[1:]
    out_ref, d_refs, o_ref, sem, *rest = refs
    _, size = o_ref.shape
    if start > known:
        u_ref, = rest
        fetch = pltpu.make_async_copy(prev_ref.at[pl.ds(known, start - known), pl.ds(start, size - start)], u_ref, sem.at[0])
        fetch.start()
    far_ref, near_ref, own_ref, *pair = parts
    own = own_sum(odd_ref, own_ref[...], pair[0][...]) if pair else own_ref[...]
    total = own + far_ref[...] + near_ref[...]
    o_ref[...] = jnp.zeros_like(o_ref)
    r = lax.broadcasted_iota(jnp.int32, (LANES, LANES), 0)
    c = lax.broadcasted_iota(jnp.int32, (LANES, LANES), 1)
    eye = jnp.where(r == c, 1.0, 0.0).astype(jnp.float32)
    if start > known:
        fetch.wait()
    puts = []
    for n, (b, at, width) in enumerate(panels(group, size)[0]):
        s = b * LANES
        top = s - start
        d_ref = d_refs.at[n % 2]

        def left_of(first, last):
            a = total[:, at + first:at + last]
            if start > known:
                a = a - exact_tn(u_ref[:, top:top + LANES], u_ref[:, top + first:top + last])
            if top:
                a = a - exact_tn(o_ref[:top, s:s + LANES], o_ref[:top, s + first:s + last])
            return a

        d_ref[:, :LANES] = left_of(0, LANES)
        d_ref[:, LANES:] = eye
        if width > LANES:
            a = left_of(LANES, width)
        factor_diag(d_ref)
        o_ref[top:top + LANES, s:s + LANES] = jnp.where(r <= c, d_ref[:, :LANES], 0.0)
        if width > LANES:
            inverse = d_ref[:, LANES:]
            o_ref[top:top + LANES, s + LANES:s + 2 * LANES] = exact_nn(inverse, a[:, :LANES])
            if width > 2 * LANES:
                o_ref[top:top + LANES, s + 2 * LANES:] = exact_nn(inverse, a[:, LANES:])
        put = pltpu.make_async_copy(o_ref.at[pl.ds(top, LANES), :], out_ref.at[pl.ds(s, LANES), :], sem.at[1 + n])
        put.start()
        puts.append(put)
    for put in puts:
        put.wait()


def factor_rows(group, known, size, odd, parts, prev):
    start, rows = group[0] * LANES, (group[1] - group[0]) * LANES
    f32 = jnp.float32
    scratch = [pltpu.VMEM((2, LANES, 2 * LANES), f32), pltpu.VMEM((rows, size), f32)]
    scratch.append(pltpu.SemaphoreType.DMA((1 + rows // LANES,)))
    in_specs = [pl.BlockSpec(memory_space=pltpu.SMEM)] + [pl.BlockSpec(memory_space=pltpu.VMEM)] * len(parts)
    args = [odd, *parts]
    aliases = {}
    if start:
        aliases = {len(args): 0}
        in_specs.append(pl.BlockSpec(memory_space=pl.ANY))
        args.append(prev)
    if start > known:
        scratch.append(pltpu.VMEM((start - known, size - start), f32))
    return pl.pallas_call(
        functools.partial(factor_kernel, group, known, len(parts)),
        out_shape=jax.ShapeDtypeStruct((size, size), f32),
        in_specs=in_specs,
        out_specs=pl.BlockSpec(memory_space=pl.ANY),
        scratch_shapes=scratch,
        input_output_aliases=aliases,
        compiler_params=pltpu.CompilerParams(vmem_limit_bytes=ROOM),
    )(*args)


def body(observations, counts, prior):
    size = observations.shape[1]
    steps = lax.axis_size("tm")
    groups = groups_of(size)
    odd = lax.rem(lax.axis_index("tm"), 2)
    swap = [(t, t ^ 1) for t in range(steps)]
    ahead = [(t, t + 3) for t in range(steps - 3)]
    inward = [(t, t - 1) for t in range(1, steps, 2)]
    owns = []
    for i, share in enumerate((groups[:1], groups[1:])):
        owns += gram_rows(share, i == 0, observations, counts, prior)
    parts = []
    for own in owns:
        pair = lax.ppermute(own, "tm", swap)
        send = jnp.where(odd == 0, own + pair, own)
        far = lax.ppermute(send, "tm", ahead)
        near = lax.ppermute(far, "tm", inward)
        parts.append([far, near, own, pair])
    factor, known = None, 0
    for i, group in enumerate(groups):
        if i == SETTLE:
            known = group[0] * LANES
            owns, pairs = zip(*(part[2:] for part in parts[i:]))
            settled = settle_rows(groups[i:], size, odd[None], owns, pairs, factor)
            parts[i:] = [[*part[:2], base] for part, base in zip(parts[i:], settled)]
        factor = factor_rows(group, known, size, odd[None], parts[i], factor)
    return factor[None]


def solution(mesh):
    placed = (P(("grp", "tm"), None), P(("grp", "tm")), P(("grp", "tm"), None))
    return jax.shard_map(
        body, mesh=mesh, in_specs=placed, out_specs=P(("grp", "tm"), None, None), check_vma=False
    )
```

```python
import functools
import jax
import jax.numpy as jnp
from jax import lax
from jax.experimental import pallas as pl
from jax.experimental.pallas import tpu as pltpu
from jax.sharding import PartitionSpec as P


LANES = 128
SUBS = 8
MICRO = 32
LEAD = 3
DEPTH = 512
ROOM = 24 << 20
CUTS = (1, 2, 4, 5)
SETTLE = 2


def parts_of(x):
    out = []
    for _ in range(3):
        out.append(x.astype(jnp.bfloat16))
        x = x - out[-1].astype(jnp.float32)
    return out


def exact_tn(a, b):
    a, b = parts_of(a), parts_of(b)
    order = ((0, 0), (0, 1), (1, 0), (1, 1), (0, 2), (2, 0))
    left = jnp.concatenate([a[i] for i, _ in order], 0)
    right = jnp.concatenate([b[j] for _, j in order], 0)
    return lax.dot_general(left, right, (((0,), (0,)), ((), ())), preferred_element_type=jnp.float32)


def exact_nn(a, b):
    a, b = parts_of(a), parts_of(b)
    order = ((0, 0), (0, 1), (1, 0), (1, 1), (0, 2), (2, 0))
    left = jnp.concatenate([a[i] for i, _ in order], 1)
    right = jnp.concatenate([b[j] for _, j in order], 0)
    return lax.dot_general(left, right, (((1,), (0,)), ((), ())), preferred_element_type=jnp.float32)


def row_of(x, i):
    return jnp.broadcast_to(x[i:i + 1, :], x.shape)


def lane_of(x, j):
    return jnp.take_along_axis(x, jnp.full(x.shape, j, jnp.int32), axis=1)


def eliminate(tiles, first):
    sub = lax.broadcasted_iota(jnp.int32, (SUBS, LANES), 0)
    groups = len(tiles)
    for p in range(groups):
        base = first + SUBS * p
        cols = [[lane_of(tiles[g][0], base + j) for g in range(p + (p > 0), groups)] for j in range(SUBS)]
        if p:
            cols = [[own, *rest] for own, rest in zip(coming, cols)]
        last = p + 1 == groups
        scale, mix = None, None
        for i in range(0, SUBS, 2):
            x, y = cols[i], cols[i + 1]
            aa, ab, bb = row_of(x[0], i), row_of(y[0], i), row_of(y[0], i + 1)
            det = aa * bb - ab * ab
            ra, rd = 1.0 / aa, 1.0 / det
            root = lax.rsqrt(aa)
            tail = aa * root * lax.rsqrt(det)
            skew = ab * ra
            scale = jnp.where(sub == i + 1, tail, root if scale is None else jnp.where(sub == i, root, scale))
            mix = jnp.where(sub == i + 1, skew, 0.0 if mix is None else mix)
            w = jnp.where(sub > i + 1, y[0] * aa - x[0] * ab, 0.0)
            z = jnp.where(sub > i + 1, x[0], 0.0)
            mx = [u * ra for u in (z, *x[1:])]
            mw = [w * rd, *((v - m * ab) * (aa * rd) for v, m in zip(y[1:], mx[1:]))]
            for j in range(i + 2, SUBS):
                own, *rest = cols[j]
                e, f = row_of(own, i), row_of(own, i + 1)
                h = f - skew * e
                if j < i + 4:
                    own = (own - (z * e) * ra) - ((w * (f * aa - e * ab)) * ra) * rd
                else:
                    own = own - mx[0] * e - mw[0] * h
                cols[j] = [own, *(c - u * e - v * h for c, u, v in zip(rest, mx[1:], mw[1:]))]
            if not last and i == SUBS - 2 * LEAD:
                coming = [lane_of(tiles[p + 1][0], base + SUBS + j) for j in range(SUBS)]
                over = [lane_of(tiles[p][0], base + SUBS + j) for j in range(SUBS)]
            if not last and i >= SUBS - 2 * LEAD:
                for j in range(SUBS):
                    e, f = row_of(over[j], i), row_of(over[j], i + 1)
                    h = f - skew * e
                    coming[j] = coming[j] - mx[1] * e - mw[1] * h
                    if i + 2 < SUBS:
                        over[j] = over[j] - mx[0] * e - mw[0] * h
            for t in range(len(tiles[p])):
                e, f = row_of(tiles[p][t], i), row_of(tiles[p][t], i + 1)
                h = f - skew * e
                for g in range(p, groups):
                    tiles[g][t] = tiles[g][t] - mx[g - p] * e - mw[g - p] * h
        for t in range(len(tiles[p])):
            v = tiles[p][t]
            tiles[p][t] = (v - mix * pltpu.roll(v, 1, 0)) * scale
    return tiles


def factor_diag(d_ref):
    n, wide = d_ref.shape
    for r0 in range(0, n, MICRO):
        tiles = [[d_ref[r0 + SUBS * g:r0 + SUBS * (g + 1), LANES * t:LANES * (t + 1)] for t in range(wide // LANES)] for g in range(MICRO // SUBS)]
        tiles = eliminate(tiles, r0)
        for g, row in enumerate(tiles):
            for t, tile in enumerate(row):
                d_ref[r0 + SUBS * g:r0 + SUBS * (g + 1), LANES * t:LANES * (t + 1)] = tile
        r1 = r0 + MICRO
        if r1 < n:
            u = d_ref[r0:r1, :]
            d_ref[r1:, :] = d_ref[r1:, :] - exact_tn(u[:, :LANES], u)[r1:]


def groups_of(size):
    edges = [0, *[c for c in CUTS if c * LANES < size], size // LANES]
    return list(zip(edges[:-1], edges[1:]))


def panels(group, size):
    at, out = 0, []
    for r in range(*group):
        width = size - r * LANES
        out.append((r, at, width))
        at += width
    return out, at


def add_grams(groups, h, out_refs):
    size = h.shape[1]
    for group, out_ref in zip(groups, out_refs):
        first, last = group[0] * LANES, group[1] * LANES
        gram = lax.dot_general(h[:, first:last], h[:, first:], (((0,), (0,)), ((), ())), preferred_element_type=jnp.float32)
        for b, at, width in panels(group, size)[0]:
            r = b * LANES - first
            out_ref[:, at:at + width] += gram[r:r + LANES, r:]


def set_priors(groups, prior_ref, out_refs):
    size = prior_ref.shape[1]
    r = lax.broadcasted_iota(jnp.int32, (LANES, LANES), 0)
    c = lax.broadcasted_iota(jnp.int32, (LANES, LANES), 1)
    for group, out_ref in zip(groups, out_refs):
        out_ref[...] = jnp.zeros_like(out_ref)
        for b, at, _ in panels(group, size)[0]:
            diag = jnp.broadcast_to(prior_ref[:, b * LANES:(b + 1) * LANES], (LANES, LANES))
            out_ref[:, at:at + LANES] = jnp.where(r == c, diag, 0.0)


def live_rows(h, left):
    index = lax.broadcasted_iota(jnp.int32, h.shape, 0)
    return jnp.where(index < left, h, jnp.zeros_like(h))


def gram_kernel(groups, fetched, count_ref, h_ref, prior_ref, *refs):
    n = len(groups)
    out_refs, refs = refs[:n], refs[n:]
    depth = min(DEPTH, h_ref.shape[0])
    pieces = h_ref.shape[0] // depth
    rows_ref = h_ref
    if fetched:
        rows_ref, bias_ref, sem = refs
        bias = pltpu.make_async_copy(prior_ref, bias_ref, sem.at[pieces])
        bias.start()

    def fetch(k):
        rows = pl.ds(k * depth, depth)
        return pltpu.make_async_copy(h_ref.at[rows, :], rows_ref.at[rows, :], sem.at[k])

    if fetched:
        for k in range(pieces):
            pl.when(k * depth < count_ref[0])(fetch(k).start)
        bias.wait()
    set_priors(groups, bias_ref if fetched else prior_ref, out_refs)
    for k in range(pieces):
        left = count_ref[0] - k * depth
        rows = slice(k * depth, (k + 1) * depth)
        if fetched:
            pl.when(left > 0)(fetch(k).wait)

        @pl.when(left >= depth)
        def _():
            add_grams(groups, rows_ref[rows, :], out_refs)

        @pl.when(jnp.logical_and(left > 0, left < depth))
        def _():
            add_grams(groups, live_rows(rows_ref[rows, :], left), out_refs)


def gram_rows(groups, fetched, observations, counts, prior):
    capacity, size = observations.shape
    totals = [panels(group, size)[1] for group in groups]
    vmem, smem = pl.BlockSpec(memory_space=pltpu.VMEM), pl.BlockSpec(memory_space=pltpu.SMEM)
    if fetched:
        observations = pltpu.with_memory_space_constraint(observations, pltpu.HBM)
        prior = pltpu.with_memory_space_constraint(prior, pltpu.HBM)
        place = pl.BlockSpec(memory_space=pltpu.HBM)
        scratch = [
            pltpu.VMEM((capacity, size), observations.dtype),
            pltpu.VMEM((1, size), prior.dtype),
            pltpu.SemaphoreType.DMA((1 + max(1, capacity // DEPTH),)),
        ]
    else:
        place, scratch = vmem, []
    return pl.pallas_call(
        functools.partial(gram_kernel, groups, fetched),
        out_shape=[jax.ShapeDtypeStruct((LANES, total), jnp.float32) for total in totals],
        in_specs=[smem, place, place],
        out_specs=[vmem] * len(groups),
        scratch_shapes=scratch,
        compiler_params=pltpu.CompilerParams(vmem_limit_bytes=ROOM),
    )(counts, observations, prior)


def own_sum(odd_ref, own, pair):
    return own + jnp.where(odd_ref[0] > 0, pair, 0.0)


def settle_kernel(groups, odd_ref, *refs):
    n = len(groups)
    owns, pairs, (factor_ref, *outs), (u_ref, sem) = refs[:n], refs[n:2 * n], refs[2 * n:-2], refs[-2:]
    known, width = u_ref.shape
    size = known + width
    fetch = pltpu.make_async_copy(factor_ref.at[pl.ds(0, known), pl.ds(known, width)], u_ref, sem)
    fetch.start()
    fetch.wait()
    for group, own_ref, pair_ref, out_ref in zip(groups, owns, pairs, outs):
        for b, at, w in panels(group, size)[0]:
            s = b * LANES - known
            part = own_sum(odd_ref, own_ref[:, at:at + w], pair_ref[:, at:at + w])
            out_ref[:, at:at + w] = part - exact_tn(u_ref[:, s:s + LANES], u_ref[:, s:])


def settle_rows(groups, size, odd, owns, pairs, factor):
    vmem, smem, f32 = pl.BlockSpec(memory_space=pltpu.VMEM), pl.BlockSpec(memory_space=pltpu.SMEM), jnp.float32
    known = groups[0][0] * LANES
    return pl.pallas_call(
        functools.partial(settle_kernel, groups),
        out_shape=[jax.ShapeDtypeStruct(own.shape, f32) for own in owns],
        in_specs=[smem] + [vmem] * (2 * len(groups)) + [pl.BlockSpec(memory_space=pl.ANY)],
        out_specs=[vmem] * len(groups),
        scratch_shapes=[pltpu.VMEM((known, size - known), f32), pltpu.SemaphoreType.DMA],
        compiler_params=pltpu.CompilerParams(vmem_limit_bytes=ROOM),
        name="settle",
    )(odd, *owns, *pairs, factor)


def factor_kernel(group, later, known, n_parts, odd_ref, *refs):
    start = group[0] * LANES
    parts, bases, refs = refs[:n_parts], refs[n_parts:n_parts + len(later)], refs[n_parts + len(later):]
    if start:
        prev_ref, refs = refs[0], refs[1:]
    out_ref, lowered, refs = refs[0], refs[1:1 + len(later)], refs[1 + len(later):]
    d_refs, o_ref, sem, *rest = refs
    _, size = o_ref.shape
    if start > known:
        u_ref, = rest
        fetch = pltpu.make_async_copy(prev_ref.at[pl.ds(known, start - known), pl.ds(start, size - start)], u_ref, sem.at[0])
        fetch.start()
    far_ref, near_ref, own_ref, *pair = parts
    own = own_sum(odd_ref, own_ref[...], pair[0][...]) if pair else own_ref[...]
    total = own + far_ref[...] + near_ref[...]
    o_ref[...] = jnp.zeros_like(o_ref)
    r = lax.broadcasted_iota(jnp.int32, (LANES, LANES), 0)
    c = lax.broadcasted_iota(jnp.int32, (LANES, LANES), 1)
    eye = jnp.where(r == c, 1.0, 0.0).astype(jnp.float32)
    if start > known:
        fetch.wait()
    puts = []
    for n, (b, at, width) in enumerate(panels(group, size)[0]):
        s = b * LANES
        top = s - start
        d_ref = d_refs.at[n % 2]

        def left_of(first, last):
            a = total[:, at + first:at + last]
            if start > known:
                a = a - exact_tn(u_ref[:, top:top + LANES], u_ref[:, top + first:top + last])
            if top:
                a = a - exact_tn(o_ref[:top, s:s + LANES], o_ref[:top, s + first:s + last])
            return a

        d_ref[:, :LANES] = left_of(0, LANES)
        if width > LANES:
            d_ref[:, LANES:] = eye
            a = left_of(LANES, width)
            factor_diag(d_ref)
        else:
            factor_diag(d_ref.at[:, pl.ds(0, LANES)])
        o_ref[top:top + LANES, s:s + LANES] = jnp.where(r <= c, d_ref[:, :LANES], 0.0)
        if width > LANES:
            inverse = d_ref[:, LANES:]
            o_ref[top:top + LANES, s + LANES:s + 2 * LANES] = exact_nn(inverse, a[:, :LANES])
            if width > 2 * LANES:
                o_ref[top:top + LANES, s + 2 * LANES:] = exact_nn(inverse, a[:, LANES:])
        put = pltpu.make_async_copy(o_ref.at[pl.ds(top, LANES), :], out_ref.at[pl.ds(s, LANES), :], sem.at[1 + n])
        put.start()
        puts.append(put)
    for below, base_ref, low_ref in zip(later, bases, lowered):
        for b, at, w in panels(below, size)[0]:
            s = b * LANES
            low_ref[:, at:at + w] = base_ref[:, at:at + w] - exact_tn(o_ref[:, s:s + LANES], o_ref[:, s:])
    for put in puts:
        put.wait()


def factor_rows(group, later, known, size, odd, parts, bases, prev):
    start, rows = group[0] * LANES, (group[1] - group[0]) * LANES
    f32 = jnp.float32
    scratch = [pltpu.VMEM((2, LANES, 2 * LANES), f32), pltpu.VMEM((rows, size), f32)]
    scratch.append(pltpu.SemaphoreType.DMA((1 + rows // LANES,)))
    in_specs = [pl.BlockSpec(memory_space=pltpu.SMEM)] + [pl.BlockSpec(memory_space=pltpu.VMEM)] * (len(parts) + len(bases))
    args = [odd, *parts, *bases]
    aliases = {}
    if start:
        aliases = {len(args): 0}
        in_specs.append(pl.BlockSpec(memory_space=pl.ANY))
        args.append(prev)
    if start > known:
        scratch.append(pltpu.VMEM((start - known, size - start), f32))
    return pl.pallas_call(
        functools.partial(factor_kernel, group, later, known, len(parts)),
        out_shape=[jax.ShapeDtypeStruct((size, size), f32)] + [jax.ShapeDtypeStruct(base.shape, f32) for base in bases],
        in_specs=in_specs,
        out_specs=[pl.BlockSpec(memory_space=pl.ANY)] + [pl.BlockSpec(memory_space=pltpu.VMEM)] * len(bases),
        scratch_shapes=scratch,
        input_output_aliases=aliases,
        compiler_params=pltpu.CompilerParams(vmem_limit_bytes=ROOM),
    )(*args)


def body(observations, counts, prior):
    size = observations.shape[1]
    steps = lax.axis_size("tm")
    groups = groups_of(size)
    odd = lax.rem(lax.axis_index("tm"), 2)
    swap = [(t, t ^ 1) for t in range(steps)]
    ahead = [(t, t + 3) for t in range(steps - 3)]
    inward = [(t, t - 1) for t in range(1, steps, 2)]
    owns = []
    for i, share in enumerate((groups[:1], groups[1:])):
        owns += gram_rows(share, i == 0, observations, counts, prior)
    parts = []
    for own in owns:
        pair = lax.ppermute(own, "tm", swap)
        send = jnp.where(odd == 0, own + pair, own)
        far = lax.ppermute(send, "tm", ahead)
        near = lax.ppermute(far, "tm", inward)
        parts.append([far, near, own, pair])
    factor, known = None, 0
    for i, group in enumerate(groups):
        if i == SETTLE:
            known = group[0] * LANES
            owns, pairs = zip(*(part[2:] for part in parts[i:]))
            settled = settle_rows(groups[i:], size, odd[None], owns, pairs, factor)
            parts[i:] = [[*part[:2], base] for part, base in zip(parts[i:], settled)]
        later = groups[i + 1:] if i >= SETTLE else []
        bases = [part[2] for part in parts[i + 1:]] if later else []
        factor, *lowered = factor_rows(group, later, known, size, odd[None], parts[i], bases, factor)
        if later:
            known = group[1] * LANES
            parts[i + 1:] = [[*part[:2], low] for part, low in zip(parts[i + 1:], lowered)]
    return factor[None]


def solution(mesh):
    placed = (P(("grp", "tm"), None), P(("grp", "tm")), P(("grp", "tm"), None))
    return jax.shard_map(
        body, mesh=mesh, in_specs=placed, out_specs=P(("grp", "tm"), None, None), check_vma=False
    )
```

```python
import functools
import jax
import jax.numpy as jnp
from jax import lax
from jax.experimental import pallas as pl
from jax.experimental.pallas import tpu as pltpu
from jax.sharding import PartitionSpec as P


LANES = 128
SUBS = 8
MICRO = 32
LEAD = 3
DEPTH = 512
ROOM = 24 << 20
CUTS = (1, 2, 4, 6)
SETTLE = 2


def parts_of(x):
    out = []
    for _ in range(3):
        out.append(x.astype(jnp.bfloat16))
        x = x - out[-1].astype(jnp.float32)
    return out


def exact_tn(a, b):
    a, b = parts_of(a), parts_of(b)
    order = ((0, 0), (0, 1), (1, 0), (1, 1), (0, 2), (2, 0))
    left = jnp.concatenate([a[i] for i, _ in order], 0)
    right = jnp.concatenate([b[j] for _, j in order], 0)
    return lax.dot_general(left, right, (((0,), (0,)), ((), ())), preferred_element_type=jnp.float32)


def exact_nn(a, b):
    a, b = parts_of(a), parts_of(b)
    order = ((0, 0), (0, 1), (1, 0), (1, 1), (0, 2), (2, 0))
    left = jnp.concatenate([a[i] for i, _ in order], 1)
    right = jnp.concatenate([b[j] for _, j in order], 0)
    return lax.dot_general(left, right, (((1,), (0,)), ((), ())), preferred_element_type=jnp.float32)


def row_of(x, i):
    return jnp.broadcast_to(x[i:i + 1, :], x.shape)


def lane_of(x, j):
    return jnp.take_along_axis(x, jnp.full(x.shape, j, jnp.int32), axis=1)


def eliminate(tiles, first):
    sub = lax.broadcasted_iota(jnp.int32, (SUBS, LANES), 0)
    groups = len(tiles)
    for p in range(groups):
        base = first + SUBS * p
        cols = [[lane_of(tiles[g][0], base + j) for g in range(p + (p > 0), groups)] for j in range(SUBS)]
        if p:
            cols = [[own, *rest] for own, rest in zip(coming, cols)]
        last = p + 1 == groups
        scale, mix = None, None
        for i in range(0, SUBS, 2):
            x, y = cols[i], cols[i + 1]
            aa, ab, bb = row_of(x[0], i), row_of(y[0], i), row_of(y[0], i + 1)
            det = aa * bb - ab * ab
            ra, rd = 1.0 / aa, 1.0 / det
            root = lax.rsqrt(aa)
            tail = aa * root * lax.rsqrt(det)
            skew = ab * ra
            scale = jnp.where(sub == i + 1, tail, root if scale is None else jnp.where(sub == i, root, scale))
            mix = jnp.where(sub == i + 1, skew, 0.0 if mix is None else mix)
            w = jnp.where(sub > i + 1, y[0] * aa - x[0] * ab, 0.0)
            z = jnp.where(sub > i + 1, x[0], 0.0)
            mx = [u * ra for u in (z, *x[1:])]
            mw = [w * rd, *((v - m * ab) * (aa * rd) for v, m in zip(y[1:], mx[1:]))]
            for j in range(i + 2, SUBS):
                own, *rest = cols[j]
                e, f = row_of(own, i), row_of(own, i + 1)
                h = f - skew * e
                if j < i + 4:
                    own = (own - (z * e) * ra) - ((w * (f * aa - e * ab)) * ra) * rd
                else:
                    own = own - mx[0] * e - mw[0] * h
                cols[j] = [own, *(c - u * e - v * h for c, u, v in zip(rest, mx[1:], mw[1:]))]
            if not last and i == SUBS - 2 * LEAD:
                coming = [lane_of(tiles[p + 1][0], base + SUBS + j) for j in range(SUBS)]
                over = [lane_of(tiles[p][0], base + SUBS + j) for j in range(SUBS)]
            if not last and i >= SUBS - 2 * LEAD:
                for j in range(SUBS):
                    e, f = row_of(over[j], i), row_of(over[j], i + 1)
                    h = f - skew * e
                    coming[j] = coming[j] - mx[1] * e - mw[1] * h
                    if i + 2 < SUBS:
                        over[j] = over[j] - mx[0] * e - mw[0] * h
            for t in range(len(tiles[p])):
                e, f = row_of(tiles[p][t], i), row_of(tiles[p][t], i + 1)
                h = f - skew * e
                for g in range(p, groups):
                    tiles[g][t] = tiles[g][t] - mx[g - p] * e - mw[g - p] * h
        for t in range(len(tiles[p])):
            v = tiles[p][t]
            tiles[p][t] = (v - mix * pltpu.roll(v, 1, 0)) * scale
    return tiles


def factor_diag(d_ref):
    n, wide = d_ref.shape
    for r0 in range(0, n, MICRO):
        tiles = [[d_ref[r0 + SUBS * g:r0 + SUBS * (g + 1), LANES * t:LANES * (t + 1)] for t in range(wide // LANES)] for g in range(MICRO // SUBS)]
        tiles = eliminate(tiles, r0)
        for g, row in enumerate(tiles):
            for t, tile in enumerate(row):
                d_ref[r0 + SUBS * g:r0 + SUBS * (g + 1), LANES * t:LANES * (t + 1)] = tile
        r1 = r0 + MICRO
        if r1 < n:
            u = d_ref[r0:r1, :]
            d_ref[r1:, :] = d_ref[r1:, :] - exact_tn(u[:, :LANES], u)[r1:]


def groups_of(size):
    edges = [0, *[c for c in CUTS if c * LANES < size], size // LANES]
    return list(zip(edges[:-1], edges[1:]))


def panels(group, size):
    at, out = 0, []
    for r in range(*group):
        width = size - r * LANES
        out.append((r, at, width))
        at += width
    return out, at


def add_grams(groups, h, out_refs):
    size = h.shape[1]
    for group, out_ref in zip(groups, out_refs):
        first, last = group[0] * LANES, group[1] * LANES
        gram = lax.dot_general(h[:, first:last], h[:, first:], (((0,), (0,)), ((), ())), preferred_element_type=jnp.float32)
        for b, at, width in panels(group, size)[0]:
            r = b * LANES - first
            out_ref[:, at:at + width] += gram[r:r + LANES, r:]


def set_priors(groups, prior_ref, out_refs):
    size = prior_ref.shape[1]
    r = lax.broadcasted_iota(jnp.int32, (LANES, LANES), 0)
    c = lax.broadcasted_iota(jnp.int32, (LANES, LANES), 1)
    for group, out_ref in zip(groups, out_refs):
        out_ref[...] = jnp.zeros_like(out_ref)
        for b, at, _ in panels(group, size)[0]:
            diag = jnp.broadcast_to(prior_ref[:, b * LANES:(b + 1) * LANES], (LANES, LANES))
            out_ref[:, at:at + LANES] = jnp.where(r == c, diag, 0.0)


def live_rows(h, left):
    index = lax.broadcasted_iota(jnp.int32, h.shape, 0)
    return jnp.where(index < left, h, jnp.zeros_like(h))


def gram_kernel(groups, fetched, count_ref, h_ref, prior_ref, *refs):
    n = len(groups)
    out_refs, refs = refs[:n], refs[n:]
    depth = min(DEPTH, h_ref.shape[0])
    pieces = h_ref.shape[0] // depth
    rows_ref = h_ref
    if fetched:
        rows_ref, bias_ref, sem = refs
        bias = pltpu.make_async_copy(prior_ref, bias_ref, sem.at[pieces])
        bias.start()

    def fetch(k):
        rows = pl.ds(k * depth, depth)
        return pltpu.make_async_copy(h_ref.at[rows, :], rows_ref.at[rows, :], sem.at[k])

    if fetched:
        for k in range(pieces):
            pl.when(k * depth < count_ref[0])(fetch(k).start)
        bias.wait()
    set_priors(groups, bias_ref if fetched else prior_ref, out_refs)
    for k in range(pieces):
        left = count_ref[0] - k * depth
        rows = slice(k * depth, (k + 1) * depth)
        if fetched:
            pl.when(left > 0)(fetch(k).wait)

        @pl.when(left >= depth)
        def _():
            add_grams(groups, rows_ref[rows, :], out_refs)

        @pl.when(jnp.logical_and(left > 0, left < depth))
        def _():
            add_grams(groups, live_rows(rows_ref[rows, :], left), out_refs)


def gram_rows(groups, fetched, observations, counts, prior):
    capacity, size = observations.shape
    totals = [panels(group, size)[1] for group in groups]
    vmem, smem = pl.BlockSpec(memory_space=pltpu.VMEM), pl.BlockSpec(memory_space=pltpu.SMEM)
    if fetched:
        observations = pltpu.with_memory_space_constraint(observations, pltpu.HBM)
        prior = pltpu.with_memory_space_constraint(prior, pltpu.HBM)
        place = pl.BlockSpec(memory_space=pltpu.HBM)
        scratch = [
            pltpu.VMEM((capacity, size), observations.dtype),
            pltpu.VMEM((1, size), prior.dtype),
            pltpu.SemaphoreType.DMA((1 + max(1, capacity // DEPTH),)),
        ]
    else:
        place, scratch = vmem, []
    return pl.pallas_call(
        functools.partial(gram_kernel, groups, fetched),
        out_shape=[jax.ShapeDtypeStruct((LANES, total), jnp.float32) for total in totals],
        in_specs=[smem, place, place],
        out_specs=[vmem] * len(groups),
        scratch_shapes=scratch,
        compiler_params=pltpu.CompilerParams(vmem_limit_bytes=ROOM),
    )(counts, observations, prior)


def own_sum(odd_ref, own, pair):
    return own + jnp.where(odd_ref[0] > 0, pair, 0.0)


def settle_kernel(groups, odd_ref, *refs):
    n = len(groups)
    owns, pairs, (factor_ref, *outs), (u_ref, sem) = refs[:n], refs[n:2 * n], refs[2 * n:-2], refs[-2:]
    known, width = u_ref.shape
    size = known + width
    fetch = pltpu.make_async_copy(factor_ref.at[pl.ds(0, known), pl.ds(known, width)], u_ref, sem)
    fetch.start()
    fetch.wait()
    for group, own_ref, pair_ref, out_ref in zip(groups, owns, pairs, outs):
        for b, at, w in panels(group, size)[0]:
            s = b * LANES - known
            part = own_sum(odd_ref, own_ref[:, at:at + w], pair_ref[:, at:at + w])
            out_ref[:, at:at + w] = part - exact_tn(u_ref[:, s:s + LANES], u_ref[:, s:])


def settle_rows(groups, size, odd, owns, pairs, factor):
    vmem, smem, f32 = pl.BlockSpec(memory_space=pltpu.VMEM), pl.BlockSpec(memory_space=pltpu.SMEM), jnp.float32
    known = groups[0][0] * LANES
    factor = pltpu.with_memory_space_constraint(factor, pltpu.HBM)
    return pl.pallas_call(
        functools.partial(settle_kernel, groups),
        out_shape=[jax.ShapeDtypeStruct(own.shape, f32) for own in owns],
        in_specs=[smem] + [vmem] * (2 * len(groups)) + [pl.BlockSpec(memory_space=pltpu.HBM)],
        out_specs=[vmem] * len(groups),
        scratch_shapes=[pltpu.VMEM((known, size - known), f32), pltpu.SemaphoreType.DMA],
        compiler_params=pltpu.CompilerParams(vmem_limit_bytes=ROOM),
        name="settle",
    )(odd, *owns, *pairs, factor)


def factor_kernel(group, later, known, n_parts, odd_ref, *refs):
    start = group[0] * LANES
    parts, bases, refs = refs[:n_parts], refs[n_parts:n_parts + len(later)], refs[n_parts + len(later):]
    if start:
        prev_ref, refs = refs[0], refs[1:]
    out_ref, lowered, refs = refs[0], refs[1:1 + len(later)], refs[1 + len(later):]
    d_refs, o_ref, sem, *rest = refs
    _, size = o_ref.shape
    if start > known:
        u_ref, = rest
        fetch = pltpu.make_async_copy(prev_ref.at[pl.ds(known, start - known), pl.ds(start, size - start)], u_ref, sem.at[0])
        fetch.start()
    far_ref, near_ref, own_ref, *pair = parts
    own = own_sum(odd_ref, own_ref[...], pair[0][...]) if pair else own_ref[...]
    total = own + far_ref[...] + near_ref[...]
    o_ref[...] = jnp.zeros_like(o_ref)
    r = lax.broadcasted_iota(jnp.int32, (LANES, LANES), 0)
    c = lax.broadcasted_iota(jnp.int32, (LANES, LANES), 1)
    eye = jnp.where(r == c, 1.0, 0.0).astype(jnp.float32)
    if start > known:
        fetch.wait()
    puts = []
    for n, (b, at, width) in enumerate(panels(group, size)[0]):
        s = b * LANES
        top = s - start
        d_ref = d_refs.at[n % 2]

        def left_of(first, last):
            a = total[:, at + first:at + last]
            if start > known:
                a = a - exact_tn(u_ref[:, top:top + LANES], u_ref[:, top + first:top + last])
            if top:
                a = a - exact_tn(o_ref[:top, s:s + LANES], o_ref[:top, s + first:s + last])
            return a

        d_ref[:, :LANES] = left_of(0, LANES)
        if width > LANES:
            d_ref[:, LANES:] = eye
            a = left_of(LANES, width)
            factor_diag(d_ref)
        else:
            factor_diag(d_ref.at[:, pl.ds(0, LANES)])
        o_ref[top:top + LANES, s:s + LANES] = jnp.where(r <= c, d_ref[:, :LANES], 0.0)
        if width > LANES:
            inverse = d_ref[:, LANES:]
            o_ref[top:top + LANES, s + LANES:s + 2 * LANES] = exact_nn(inverse, a[:, :LANES])
            if width > 2 * LANES:
                o_ref[top:top + LANES, s + 2 * LANES:] = exact_nn(inverse, a[:, LANES:])
        put = pltpu.make_async_copy(o_ref.at[pl.ds(top, LANES), :], out_ref.at[pl.ds(s, LANES), :], sem.at[1 + n])
        put.start()
        puts.append(put)
    for below, base_ref, low_ref in zip(later, bases, lowered):
        for b, at, w in panels(below, size)[0]:
            s = b * LANES
            low_ref[:, at:at + w] = base_ref[:, at:at + w] - exact_tn(o_ref[:, s:s + LANES], o_ref[:, s:])
    for put in puts:
        put.wait()


def factor_rows(group, later, known, size, odd, parts, bases, prev):
    start, rows = group[0] * LANES, (group[1] - group[0]) * LANES
    f32 = jnp.float32
    scratch = [pltpu.VMEM((2, LANES, 2 * LANES), f32), pltpu.VMEM((rows, size), f32)]
    scratch.append(pltpu.SemaphoreType.DMA((1 + rows // LANES,)))
    in_specs = [pl.BlockSpec(memory_space=pltpu.SMEM)] + [pl.BlockSpec(memory_space=pltpu.VMEM)] * (len(parts) + len(bases))
    args = [odd, *parts, *bases]
    aliases = {}
    if start:
        aliases = {len(args): 0}
        in_specs.append(pl.BlockSpec(memory_space=pl.ANY))
        args.append(prev)
    if start > known:
        scratch.append(pltpu.VMEM((start - known, size - start), f32))
    return pl.pallas_call(
        functools.partial(factor_kernel, group, later, known, len(parts)),
        out_shape=[jax.ShapeDtypeStruct((size, size), f32)] + [jax.ShapeDtypeStruct(base.shape, f32) for base in bases],
        in_specs=in_specs,
        out_specs=[pl.BlockSpec(memory_space=pl.ANY)] + [pl.BlockSpec(memory_space=pltpu.VMEM)] * len(bases),
        scratch_shapes=scratch,
        input_output_aliases=aliases,
        compiler_params=pltpu.CompilerParams(vmem_limit_bytes=ROOM),
    )(*args)


def body(observations, counts, prior):
    size = observations.shape[1]
    steps = lax.axis_size("tm")
    groups = groups_of(size)
    odd = lax.rem(lax.axis_index("tm"), 2)
    swap = [(t, t ^ 1) for t in range(steps)]
    ahead = [(t, t + 3) for t in range(steps - 3)]
    inward = [(t, t - 1) for t in range(1, steps, 2)]
    owns = []
    for i, share in enumerate((groups[:1], groups[1:])):
        owns += gram_rows(share, i == 0, observations, counts, prior)
    parts = []
    for own in owns:
        pair = lax.ppermute(own, "tm", swap)
        send = jnp.where(odd == 0, own + pair, own)
        far = lax.ppermute(send, "tm", ahead)
        near = lax.ppermute(far, "tm", inward)
        parts.append([far, near, own, pair])
    factor, known = None, 0
    for i, group in enumerate(groups):
        if i == SETTLE:
            known = group[0] * LANES
            owns, pairs = zip(*(part[2:] for part in parts[i:]))
            settled = settle_rows(groups[i:], size, odd[None], owns, pairs, factor)
            parts[i:] = [[*part[:2], base] for part, base in zip(parts[i:], settled)]
        later = groups[i + 1:] if i >= SETTLE else []
        bases = [part[2] for part in parts[i + 1:]] if later else []
        factor, *lowered = factor_rows(group, later, known, size, odd[None], parts[i], bases, factor)
        if later:
            known = group[1] * LANES
            parts[i + 1:] = [[*part[:2], low] for part, low in zip(parts[i + 1:], lowered)]
    return factor[None]


def solution(mesh):
    placed = (P(("grp", "tm"), None), P(("grp", "tm")), P(("grp", "tm"), None))
    return jax.shard_map(
        body, mesh=mesh, in_specs=placed, out_specs=P(("grp", "tm"), None, None), check_vma=False
    )
```
